32 devices in a mesh: chan: 8 (over z, x), tm: 4 (over y, core).
Axes of the slice: x: 2, y: 2, z: 4, core: 2. Of those that a mesh axis runs over, the one named last changes fastest.
Arguments:
- volts: bfloat16 [8, 64, 2, 98304], P('chan', None, None, 'tm'), may hold values from -6 to 6
- scales: float32 [8, 64, 384], P('chan', None, 'tm'), may hold values from 0.25 to 4
- dm_rate: int32 [8, 16, 2], replicated, may hold values from 8192 to 16384
Outputs:
- dedispersed: bfloat16 [64, 8, 2, 98304], P('chan', None, None, 'tm')
The draws below stay inside these ranges and needn't reach their ends.
All inputs are finite; a program needn't handle non-finite values.
Results may differ from the reference program's by a relative error of at most 0.0083.
Values may be sent and summed in bfloat16 or wider, within the bound.
A program may use at most 128 MiB of HBM per device.

```python
import math
import jax
import jax.numpy as jnp
from jax import lax

RADIX_A = 128
RADIX_B = 256
NFFT = 32768
INTERSECTION = 8192
SEGMENT = 24576
BLOCK = 256
BEAMS = 16
CHAN_DEV = 2
CHAN_BLOCKS = 8
LANES = 64
TIMES = 98304
NBLOCKS = 384
N_TM = 4


def plant(values, rng, smallest, high):
    shape = values.shape
    index_at = [jax.random.randint(jax.random.fold_in(rng, axis), (), 0, shape[axis]) for axis in range(len(shape))]
    values = values.at[tuple(index_at)].set(smallest)
    longest = shape.index(max(shape))
    index_at[longest] = (index_at[longest] + 1) % shape[longest]
    return values.at[tuple(index_at)].set(high)


def block_scale(stream_key, shape, cuts, low, top_value):
    loudness = 1.0
    for axis_at, shards_of in cuts:
        heights = jax.random.uniform(jax.random.fold_in(jax.random.fold_in(stream_key, 6), axis_at), (shards_of,), jnp.float32, low / len(cuts), top_value / len(cuts))
        loudness = loudness * jnp.repeat(jnp.exp(heights), shape[axis_at] // shards_of).reshape((-1,) + (1,) * (len(shape) - 1 - axis_at))
    return loudness


def gaussian(stream_key, dims, width, most, split=(), kind=jnp.bfloat16):
    drawn = width * jax.random.normal(stream_key, dims, jnp.float32)
    if split:
        drawn = drawn * block_scale(stream_key, dims, split, -0.22, 0.18)
    return jnp.clip(drawn, -most, most).astype(kind)


def setup_inputs(seed: int = 0) -> dict:
    seeds = jax.random.split(jax.random.key(seed), 4)
    return {
        "volts": gaussian(seeds[0], (CHAN_BLOCKS, LANES, 2, TIMES), 1.0, 6.0, ((0, 8), (3, 4))),
        "scales": jnp.clip(jnp.exp(math.log(4.0) - 2.7725887 * jax.random.uniform(seeds[1], (CHAN_BLOCKS, LANES, NBLOCKS), jnp.float32) ** block_scale(seeds[1], (CHAN_BLOCKS, LANES, NBLOCKS), ((0, 8), (2, 4)), -0.2, 0.2)), 0.25, 4.0),
        "dm_rate": plant(jax.random.randint(seeds[2], (CHAN_BLOCKS, BEAMS, CHAN_DEV), INTERSECTION, 2 * INTERSECTION + 1), jax.random.fold_in(seeds[2], 1), INTERSECTION, 2 * INTERSECTION).astype(jnp.int32),
    }


def dft_parts(radix):
    row_index = lax.broadcasted_iota(jnp.int32, (radix, radix), 0)
    col_index = lax.broadcasted_iota(jnp.int32, (radix, radix), 1)
    angle = (2.0 * math.pi / radix) * ((row_index * col_index) % radix).astype(jnp.float32)
    return jnp.cos(angle).astype(jnp.bfloat16), (-jnp.sin(angle)).astype(jnp.bfloat16)


def twiddle_parts():
    length = RADIX_A * RADIX_B
    row_index = lax.broadcasted_iota(jnp.int32, (RADIX_A, RADIX_B), 0)
    col_index = lax.broadcasted_iota(jnp.int32, (RADIX_A, RADIX_B), 1)
    angle = (2.0 * math.pi / length) * ((row_index * col_index) % length).astype(jnp.float32)
    return jnp.cos(angle), -jnp.sin(angle)


def chirp_parts(rates):
    length = RADIX_A * RADIX_B
    row_index = lax.broadcasted_iota(jnp.int32, (RADIX_A, RADIX_B), 0)
    col_index = lax.broadcasted_iota(jnp.int32, (RADIX_A, RADIX_B), 1)
    frequency = row_index + RADIX_A * col_index
    distance = jnp.abs((frequency + length // 2) % length - length // 2)
    upper_part = distance // RADIX_B
    lower_part = distance % RADIX_B
    delay_term = (length - (frequency * (INTERSECTION // 2)) % length) % length
    rate_grid = rates.reshape(-1, 1, 1)
    first_term = (rate_grid * upper_part * upper_part) % (4 * RADIX_A * RADIX_A)
    second_term = (rate_grid * upper_part * lower_part) % (2 * RADIX_A * RADIX_A * RADIX_B)
    third_term = rate_grid * lower_part * lower_part
    turns = first_term.astype(jnp.float32) / (4.0 * RADIX_A * RADIX_A)
    turns = turns + second_term.astype(jnp.float32) / (2.0 * RADIX_A * RADIX_A * RADIX_B)
    turns = turns + third_term.astype(jnp.float32) / (4.0 * length * length)
    turns = turns + delay_term.astype(jnp.float32) / (1.0 * length)
    angle = (2.0 * math.pi) * turns
    return jnp.cos(angle), jnp.sin(angle)


def to_bfloat(values):
    return lax.optimization_barrier(values.astype(jnp.bfloat16)).astype(jnp.float32)


def left_apply(matrix, array):
    return jnp.einsum("kn,snb->skb", matrix, array)


def right_apply(array, matrix):
    return jnp.einsum("skn,nm->skm", array, matrix)


def dedisperse(segments, rates):
    streams = segments.shape[0]
    head_rows = INTERSECTION // RADIX_B
    data = segments.reshape(streams, 2, RADIX_A, RADIX_B).astype(jnp.float32)
    left_re, left_im = dft_parts(RADIX_A)
    right_re, right_im = dft_parts(RADIX_B)
    left_re = left_re.astype(jnp.float32)
    left_im = left_im.astype(jnp.float32)
    right_re = right_re.astype(jnp.float32)
    right_im = right_im.astype(jnp.float32)
    twist_re, twist_im = twiddle_parts()
    real_in, imag_in = data[:, 0], data[:, 1]
    section_re = left_apply(left_re, real_in) - left_apply(left_im, imag_in)
    section_im = left_apply(left_im, real_in) + left_apply(left_re, imag_in)
    turned_re = to_bfloat(section_re * twist_re - section_im * twist_im)
    turned_im = to_bfloat(section_re * twist_im + section_im * twist_re)
    spec_re = right_apply(turned_re, right_re) - right_apply(turned_im, right_im)
    spec_im = right_apply(turned_re, right_im) + right_apply(turned_im, right_re)
    chirp_re, chirp_im = chirp_parts(rates)
    shaped_re = to_bfloat(spec_re * chirp_re - spec_im * chirp_im)
    shaped_im = to_bfloat(spec_re * chirp_im + spec_im * chirp_re)
    back_re = right_apply(shaped_re, right_re) + right_apply(shaped_im, right_im)
    back_im = right_apply(shaped_im, right_re) - right_apply(shaped_re, right_im)
    untwist_re = to_bfloat(back_re * twist_re + back_im * twist_im)
    untwist_im = to_bfloat(back_im * twist_re - back_re * twist_im)
    out_re = left_apply(left_re, untwist_re) + left_apply(left_im, untwist_im)
    out_im = left_apply(left_re, untwist_im) - left_apply(left_im, untwist_re)
    scale_back = 1.0 / (RADIX_A * RADIX_B)
    result = jnp.stack([out_re, out_im], axis=1)[:, :, head_rows:, :] * scale_back
    return result.reshape(streams, 2, SEGMENT).astype(jnp.bfloat16)


def reference(volts, scales, dm_rate):
    rate_table = jnp.repeat(dm_rate.reshape(CHAN_BLOCKS, BEAMS * CHAN_DEV), 2, axis=1)

    def one_lane(lane_index):
        lane_block = lax.dynamic_index_in_dim(volts, lane_index, 1, keepdims=False)
        lane_scales = lax.dynamic_index_in_dim(scales, lane_index, 1, keepdims=False)
        scaled = lane_block.reshape(CHAN_BLOCKS, 2, NBLOCKS, BLOCK).astype(jnp.float32) * lane_scales[:, None, :, None]
        values = scaled.reshape(CHAN_BLOCKS, 2, TIMES).astype(jnp.bfloat16)
        pieces = values.reshape(CHAN_BLOCKS, 2, N_TM, SEGMENT)
        tails = pieces[:, :, :, SEGMENT - INTERSECTION:]
        prior = jnp.concatenate([jnp.zeros_like(tails[:, :, :1]), tails[:, :, :-1]], axis=2)
        joined = jnp.concatenate([prior, pieces], axis=3)
        joined = jnp.transpose(joined, (0, 2, 1, 3)).reshape(CHAN_BLOCKS * N_TM, 2, NFFT)
        lane_rates = lax.dynamic_index_in_dim(rate_table, lane_index, 1, keepdims=False)
        stream_rates = jnp.repeat(lane_rates, N_TM)
        cleaned = dedisperse(joined, stream_rates).reshape(CHAN_BLOCKS, N_TM, 2, SEGMENT)
        return jnp.transpose(cleaned, (0, 2, 1, 3)).reshape(CHAN_BLOCKS, 2, TIMES)

    return lax.map(one_lane, jnp.arange(LANES, dtype=jnp.int32))
```

```python
import functools
import math

import jax
import jax.numpy as jnp
import ml_dtypes
import numpy as np
from jax import lax
from jax.experimental import pallas as pl
from jax.experimental.pallas import tpu as pltpu
from jax.sharding import PartitionSpec as P

RADIX_A = 128
RADIX_B = 256
NFFT = RADIX_A * RADIX_B
INTERSECTION = 8192
LANE = 128
HALVES = RADIX_B // LANE
PRIOR = INTERSECTION // LANE * 2
MESH = pl.DeviceIdType.MESH


def dft_parts(radix):
    index = np.arange(radix)
    angle = 2.0 * np.pi / radix * (np.outer(index, index) % radix)
    rounded = lambda x: x.astype(np.float32).astype(ml_dtypes.bfloat16).astype(np.float32)
    return rounded(np.cos(angle)), rounded(-np.sin(angle))


def tables():
    are, aim = dft_parts(RADIX_A)
    bre, bim = dft_parts(RADIX_B)
    eye = np.eye(HALVES, dtype=np.float32)
    left = np.array([[are, -aim], [aim, are]])
    left = np.einsum("dckn,hg->hdkngc", left, eye).reshape(HALVES * 2 * RADIX_A, -1)
    back = np.array([[are, aim], [-aim, are]]) / NFFT
    back = np.einsum("dcnk,hg->nhdgck", back, eye).reshape(-1, HALVES * 2 * RADIX_A)
    back = back[PRIOR:]
    right = np.array([[bre, bim], [-bim, bre]])
    right = right.transpose(0, 2, 1, 3).reshape(2 * RADIX_B, 2 * RADIX_B)
    unright = np.array([[bre, -bim], [bim, bre]])
    unright = unright.transpose(0, 2, 1, 3).reshape(2 * RADIX_B, 2 * RADIX_B)
    turn = np.outer(np.arange(RADIX_A), np.arange(RADIX_B)) % NFFT
    angle = 2.0 * np.pi / NFFT * turn
    twist = np.stack([np.cos(angle), -np.sin(angle)]).astype(np.float32)
    half = lambda x: x.astype(ml_dtypes.bfloat16)
    return half(left), half(right), half(unright), half(back), twist


def chirp(rate):
    shape = (RADIX_A, RADIX_B)
    k = lax.broadcasted_iota(jnp.int32, shape, 0) + RADIX_A * lax.broadcasted_iota(jnp.int32, shape, 1)
    g = jnp.minimum(k, NFFT - k)
    phase = rate * (g * g) - (k << 29)
    quarter = (phase + (1 << 29)) >> 30
    x = (phase - (quarter << 30)).astype(jnp.float32) * (2.0 * math.pi / 2.0**32)
    y = x * x
    s = x + x * y * (-1.6666654611e-1 + y * (8.3321608736e-3 + y * -1.9515295891e-4))
    c = 1.0 + y * (-0.5 + y * (4.166664568298827e-2 + y * (-1.388731625493765e-3 + y * 2.443315711809948e-5)))
    odd = (quarter & 1) == 1
    re = jnp.where(odd, s, c)
    im = jnp.where(odd, c, s)
    re = jnp.where(((quarter + 1) & 2) == 2, -re, re)
    im = jnp.where((quarter & 2) == 2, -im, im)
    return re, im


def bitwise_xor(a, b, bits):
    total = 0
    for i in range(bits):
        total = total + (a // 2**i + b // 2**i) % 2 * 2**i
    return total


def kernel(n, n_tm, own, width, rates, scales, volts, left_in, right_in, unright_in, back_in, twist_in,
           out, values, got, tail, left, right, unright, back, twist, square, spread,
           load_sem, table_sem, send_sem, recv_sem, tail_send, tail_recv):
    me = lax.axis_index("chan")
    tm = lax.axis_index("tm")
    groups = own // width
    items = n * groups
    rows = values.shape[1]
    bits = (n - 1).bit_length()

    def place(i):
        return i // n, bitwise_xor(me, i % n, bits)

    def load(i):
        g, peer = place(i)
        at = pl.ds(peer * own + g * width, width)
        return pltpu.make_async_copy(volts.at[at], values.at[at], load_sem.at[i])

    fills = [
        pltpu.make_async_copy(src, dst, table_sem.at[j])
        for j, (src, dst) in enumerate(
            [(left_in, left), (twist_in, twist), (right_in, right), (unright_in, unright), (back_in, back)]
        )
    ]

    barrier = pltpu.get_barrier_semaphore()

    @pl.loop(1, n)
    def _(r):
        pl.semaphore_signal(barrier, inc=1, device_id={"chan": bitwise_xor(me, r, bits)}, device_id_type=MESH)

    pl.semaphore_signal(barrier, inc=1, device_id={"tm": (tm + n_tm - 1) % n_tm}, device_id_type=MESH)
    pl.semaphore_signal(barrier, inc=1, device_id={"tm": (tm + 1) % n_tm}, device_id_type=MESH)

    @pl.loop(0, items)
    def _(i):
        load(i).start()

    for fill in fills:
        fill.start()

    lanes, count = scales.shape
    square[...] = jnp.zeros_like(square)
    square[0:lanes, 0:count] = scales[...]
    flipped = square[...].T[0:count]
    for j in range(rows // count):
        spread[pl.ds(j, count, stride=rows // count), :] = flipped

    pl.semaphore_wait(barrier, n + 1)

    def exchange(i):
        g, peer = place(i)
        return pltpu.make_async_remote_copy(
            src_ref=values.at[pl.ds(peer * own + g * width, width)],
            dst_ref=got.at[me, pl.ds(g * width, width)],
            send_sem=send_sem.at[i],
            recv_sem=recv_sem.at[i],
            device_id={"chan": peer},
            device_id_type=MESH,
        )

    def forward(i):
        g, peer = place(i)
        return pltpu.make_async_remote_copy(
            src_ref=got.at[peer, pl.ds(g * width, width), pl.ds(rows - PRIOR, PRIOR)],
            dst_ref=tail.at[peer, pl.ds(g * width, width)],
            send_sem=tail_send.at[i],
            recv_sem=tail_recv.at[i],
            device_id={"tm": tm + 1},
            device_id_type=MESH,
        )

    @pl.loop(0, items)
    def _(i):
        g, peer = place(i)
        load(i).wait()
        first = peer * own + g * width
        turned = pltpu.roll(spread[...], (LANE - first) % LANE, 1)
        for s in range(width):
            scale = jnp.broadcast_to(turned[:, s : s + 1], (rows, LANE))
            scaled = (values[first + s].astype(jnp.float32) * scale).astype(jnp.bfloat16)

            @pl.when(i % n > 0)
            def _():
                values[first + s] = scaled

            @pl.when(i % n == 0)
            def _():
                got[me, g * width + s] = scaled

        @pl.when(i % n > 0)
        def _():
            exchange(i).start()

    @pl.when(tm == 0)
    def _():
        @pl.loop(0, n)
        def _(c):
            tail[c] = jnp.zeros(tail.shape[1:], tail.dtype)

    for fill in fills:
        fill.wait()

    def advance(i):
        @pl.when(i % n > 0)
        def _():
            exchange(i).wait_recv()

        @pl.when(tm < n_tm - 1)
        def _():
            forward(i).start()

    advance(0)

    @pl.loop(0, items)
    def _(i):
        @pl.when(i + 1 < items)
        def _():
            advance(i + 1)

        @pl.when(tm > 0)
        def _():
            forward(i).wait_recv()

        g, c = place(i)
        base = g * width
        lane = me * own + base
        rate = rates[c, lane // 2 % 2, lane // 4]
        cre, cim = chirp(rate)
        wre, wim = twist[0], twist[1]
        streams = [
            jnp.concatenate([tail[c, base + s], got[c, base + s]], axis=0) for s in range(width)
        ]
        section = jnp.dot(
            left[...], jnp.concatenate(streams, axis=1), preferred_element_type=jnp.float32
        )
        ups = []
        for s in range(width):
            cols = slice(s * LANE, (s + 1) * LANE)
            part = lambda d: jnp.concatenate(
                [section[(h * 2 + d) * RADIX_A : (h * 2 + d + 1) * RADIX_A, cols] for h in range(HALVES)], axis=1
            )
            sre, sim = part(0), part(1)
            turned = jnp.concatenate(
                [(sre * wre - sim * wim).astype(jnp.bfloat16), (sre * wim + sim * wre).astype(jnp.bfloat16)], axis=1
            )
            spec = jnp.dot(turned, right[...], preferred_element_type=jnp.float32)
            sre, sim = spec[:, :RADIX_B], spec[:, RADIX_B:]
            shaped = jnp.concatenate(
                [(sre * cre - sim * cim).astype(jnp.bfloat16), (sre * cim + sim * cre).astype(jnp.bfloat16)], axis=1
            )
            spun = jnp.dot(shaped, unright[...], preferred_element_type=jnp.float32)
            sre, sim = spun[:, :RADIX_B], spun[:, RADIX_B:]
            ure = (sre * wre + sim * wim).astype(jnp.bfloat16)
            uim = (sim * wre - sre * wim).astype(jnp.bfloat16)
            pieces = []
            for h in range(HALVES):
                pieces += [ure[:, h * LANE : (h + 1) * LANE], uim[:, h * LANE : (h + 1) * LANE]]
            ups.append(jnp.concatenate(pieces, axis=0))
        result = jnp.dot(
            back[...], jnp.concatenate(ups, axis=1), preferred_element_type=jnp.float32
        ).astype(jnp.bfloat16)
        for s in range(width):
            out[base + s, c] = result[:, s * LANE : (s + 1) * LANE]

    @pl.loop(0, items)
    def _(i):
        @pl.when(i % n > 0)
        def _():
            exchange(i).wait_send()

        @pl.when(tm < n_tm - 1)
        def _():
            forward(i).wait_send()


def body(volts, scales, dm_rate):
    lanes, seg_len = volts.shape[1], volts.shape[3]
    count = scales.shape[2]
    n, n_tm = lax.axis_size("chan"), lax.axis_size("tm")
    own = lanes // n
    width = 2 if own % 2 == 0 else 1
    rows = seg_len // LANE * 2
    values = volts.reshape(lanes, 2, seg_len // LANE, LANE).transpose(0, 2, 1, 3).reshape(lanes, rows, LANE)
    left, right, unright, back, twist = tables()
    items = n * (own // width)
    vmem = pl.BlockSpec(memory_space=pltpu.VMEM)
    dma = pltpu.SemaphoreType.DMA
    out = pl.pallas_call(
        functools.partial(kernel, n, n_tm, own, width),
        out_shape=jax.ShapeDtypeStruct((own, n, rows, LANE), jnp.bfloat16),
        in_specs=[pl.BlockSpec(memory_space=pltpu.SMEM), vmem] + [pl.BlockSpec(memory_space=pltpu.MemorySpace.HBM)] * 6,
        out_specs=vmem,
        scratch_shapes=[
            pltpu.VMEM((lanes, rows, LANE), jnp.bfloat16),
            pltpu.VMEM((n, own, rows, LANE), jnp.bfloat16),
            pltpu.VMEM((n, own, PRIOR, LANE), jnp.bfloat16),
        ]
        + [pltpu.VMEM(x.shape, x.dtype) for x in (left, right, unright, back, twist)]
        + [
            pltpu.VMEM((LANE, LANE), jnp.float32),
            pltpu.VMEM((rows, LANE), jnp.float32),
            dma((items,)),
            dma((5,)),
            dma((items,)),
            dma((items,)),
            dma((items,)),
            dma((items,)),
        ],
        compiler_params=pltpu.CompilerParams(
            collective_id=0, has_side_effects=True, vmem_limit_bytes=56 * 2**20
        ),
        name="dedisperse",
    )(dm_rate.transpose(0, 2, 1), scales.reshape(lanes, count), values, left, right, unright, back, twist)
    out = out.reshape(own, n, seg_len // LANE, 2, LANE).transpose(0, 1, 3, 2, 4)
    return out.reshape(own, n, 2, seg_len)


def solution(mesh):
    return jax.shard_map(
        body,
        mesh=mesh,
        in_specs=(P("chan", None, None, "tm"), P("chan", None, "tm"), P()),
        out_specs=P("chan", None, None, "tm"),
        check_vma=False,
    )
```

```python
import functools
import math

import jax
import jax.numpy as jnp
import ml_dtypes
import numpy as np
from jax import lax
from jax.experimental import pallas as pl
from jax.experimental.pallas import tpu as pltpu
from jax.sharding import PartitionSpec as P

RADIX_A = 128
RADIX_B = 256
NFFT = RADIX_A * RADIX_B
INTERSECTION = 8192
LANE = 128
HALVES = RADIX_B // LANE
PRIOR = INTERSECTION // LANE * 2
MESH = pl.DeviceIdType.MESH


def dft_parts(radix):
    index = np.arange(radix)
    angle = 2.0 * np.pi / radix * (np.outer(index, index) % radix)
    rounded = lambda x: x.astype(np.float32).astype(ml_dtypes.bfloat16).astype(np.float32)
    return rounded(np.cos(angle)), rounded(-np.sin(angle))


def tables():
    are, aim = dft_parts(RADIX_A)
    bre, bim = dft_parts(RADIX_B)
    eye = np.eye(HALVES, dtype=np.float32)
    left = np.array([[are, -aim], [aim, are]])
    left = np.einsum("dckn,hg->hdkngc", left, eye).reshape(HALVES * 2 * RADIX_A, -1)
    back = np.array([[are, aim], [-aim, are]]) / NFFT
    back = np.einsum("dcnk,hg->nhdgck", back, eye).reshape(-1, HALVES * 2 * RADIX_A)
    back = back[PRIOR:]
    right = np.array([[bre, bim], [-bim, bre]])
    right = right.transpose(0, 2, 1, 3).reshape(2 * RADIX_B, 2 * RADIX_B)
    unright = np.array([[bre, -bim], [bim, bre]])
    unright = unright.transpose(0, 2, 1, 3).reshape(2 * RADIX_B, 2 * RADIX_B)
    turn = np.outer(np.arange(RADIX_A), np.arange(RADIX_B)) % NFFT
    angle = 2.0 * np.pi / NFFT * turn
    twist = np.stack([np.cos(angle), -np.sin(angle)]).astype(np.float32)
    half = lambda x: x.astype(ml_dtypes.bfloat16)
    return half(left), half(right), half(unright), half(back), twist


def chirp(rate):
    shape = (RADIX_A, RADIX_B)
    k = lax.broadcasted_iota(jnp.int32, shape, 0) + RADIX_A * lax.broadcasted_iota(jnp.int32, shape, 1)
    g = jnp.minimum(k, NFFT - k)
    phase = rate * (g * g) - (k << 29)
    quarter = (phase + (1 << 29)) >> 30
    x = (phase - (quarter << 30)).astype(jnp.float32) * (2.0 * math.pi / 2.0**32)
    y = x * x
    s = x + x * y * (-1.6666654611e-1 + y * (8.3321608736e-3 + y * -1.9515295891e-4))
    c = 1.0 + y * (-0.5 + y * (4.166664568298827e-2 + y * (-1.388731625493765e-3 + y * 2.443315711809948e-5)))
    odd = (quarter & 1) == 1
    re = jnp.where(odd, s, c)
    im = jnp.where(odd, c, s)
    re = jnp.where(((quarter + 1) & 2) == 2, -re, re)
    im = jnp.where((quarter & 2) == 2, -im, im)
    return re, im


def bitwise_xor(a, b, bits):
    total = 0
    for i in range(bits):
        total = total + (a // 2**i + b // 2**i) % 2 * 2**i
    return total


def kernel(n, n_tm, own, width, rates, scales, volts, left_in, right_in, unright_in, back_in, twist_in,
           out, values, got, tail, left, right, unright, back, twist, square, spread,
           load_sem, table_sem, send_sem, recv_sem, tail_send, tail_recv):
    me = lax.axis_index("chan")
    tm = lax.axis_index("tm")
    groups = own // width
    items = n * groups
    rows = values.shape[1]
    bits = (n - 1).bit_length()

    def place(i):
        return i // n, bitwise_xor(me, i % n, bits)

    def load(i):
        g, peer = place(i)
        at = pl.ds(peer * own + g * width, width)
        return pltpu.make_async_copy(volts.at[at], values.at[at], load_sem.at[i])

    fills = [
        pltpu.make_async_copy(src, dst, table_sem.at[j])
        for j, (src, dst) in enumerate(
            [(left_in, left), (twist_in, twist), (right_in, right), (unright_in, unright), (back_in, back)]
        )
    ]

    barrier = pltpu.get_barrier_semaphore()

    @pl.loop(1, n)
    def _(r):
        pl.semaphore_signal(barrier, inc=1, device_id={"chan": bitwise_xor(me, r, bits)}, device_id_type=MESH)

    pl.semaphore_signal(barrier, inc=1, device_id={"tm": (tm + n_tm - 1) % n_tm}, device_id_type=MESH)
    pl.semaphore_signal(barrier, inc=1, device_id={"tm": (tm + 1) % n_tm}, device_id_type=MESH)

    @pl.loop(0, items)
    def _(i):
        load(i).start()

    for fill in fills:
        fill.start()

    lanes, count = scales.shape
    square[...] = jnp.zeros_like(square)
    square[0:lanes, 0:count] = scales[...]
    flipped = square[...].T[0:count]
    for j in range(rows // count):
        spread[pl.ds(j, count, stride=rows // count), :] = flipped

    pl.semaphore_wait(barrier, n + 1)

    def exchange(i):
        g, peer = place(i)
        return pltpu.make_async_remote_copy(
            src_ref=values.at[pl.ds(peer * own + g * width, width)],
            dst_ref=got.at[me, pl.ds(g * width, width)],
            send_sem=send_sem.at[i],
            recv_sem=recv_sem.at[i],
            device_id={"chan": peer},
            device_id_type=MESH,
        )

    def forward(i):
        g, peer = place(i)
        return pltpu.make_async_remote_copy(
            src_ref=got.at[peer, pl.ds(g * width, width), pl.ds(rows - PRIOR, PRIOR)],
            dst_ref=tail.at[peer, pl.ds(g * width, width)],
            send_sem=tail_send.at[i],
            recv_sem=tail_recv.at[i],
            device_id={"tm": tm + 1},
            device_id_type=MESH,
        )

    @pl.loop(0, items)
    def _(i):
        g, peer = place(i)
        load(i).wait()
        first = peer * own + g * width
        turned = pltpu.roll(spread[...], (LANE - first) % LANE, 1)
        for s in range(width):
            scale = jnp.broadcast_to(turned[:, s : s + 1], (rows, LANE))
            scaled = (values[first + s].astype(jnp.float32) * scale).astype(jnp.bfloat16)

            @pl.when(i % n > 0)
            def _():
                values[first + s] = scaled

            @pl.when(i % n == 0)
            def _():
                got[me, g * width + s] = scaled

        @pl.when(i % n > 0)
        def _():
            exchange(i).start()

    @pl.when(tm == 0)
    def _():
        @pl.loop(0, n)
        def _(c):
            tail[c] = jnp.zeros(tail.shape[1:], tail.dtype)

    for fill in fills:
        fill.wait()

    def advance(i):
        @pl.when(i % n > 0)
        def _():
            exchange(i).wait_recv()

        @pl.when(tm < n_tm - 1)
        def _():
            forward(i).start()

    advance(0)

    @pl.loop(0, items)
    def _(i):
        @pl.when(i + 1 < items)
        def _():
            advance(i + 1)

        @pl.when(tm > 0)
        def _():
            forward(i).wait_recv()

        g, c = place(i)
        base = g * width
        lane = me * own + base
        rate = rates[c, lane // 2 % 2, lane // 4]
        cre, cim = chirp(rate)
        wre, wim = twist[0], twist[1]
        streams = [
            jnp.concatenate([tail[c, base + s], got[c, base + s]], axis=0) for s in range(width)
        ]
        section = jnp.dot(
            left[...], jnp.concatenate(streams, axis=1), preferred_element_type=jnp.float32
        )
        ups = []
        for s in range(width):
            cols = slice(s * LANE, (s + 1) * LANE)
            part = lambda d: jnp.concatenate(
                [section[(h * 2 + d) * RADIX_A : (h * 2 + d + 1) * RADIX_A, cols] for h in range(HALVES)], axis=1
            )
            sre, sim = part(0), part(1)
            turned = jnp.concatenate(
                [(sre * wre - sim * wim).astype(jnp.bfloat16), (sre * wim + sim * wre).astype(jnp.bfloat16)], axis=1
            )
            spec = jnp.dot(turned, right[...], preferred_element_type=jnp.float32)
            sre, sim = spec[:, :RADIX_B], spec[:, RADIX_B:]
            shaped = jnp.concatenate(
                [(sre * cre - sim * cim).astype(jnp.bfloat16), (sre * cim + sim * cre).astype(jnp.bfloat16)], axis=1
            )
            spun = jnp.dot(shaped, unright[...], preferred_element_type=jnp.float32)
            sre, sim = spun[:, :RADIX_B], spun[:, RADIX_B:]
            ure = (sre * wre + sim * wim).astype(jnp.bfloat16)
            uim = (sim * wre - sre * wim).astype(jnp.bfloat16)
            pieces = []
            for h in range(HALVES):
                pieces += [ure[:, h * LANE : (h + 1) * LANE], uim[:, h * LANE : (h + 1) * LANE]]
            ups.append(jnp.concatenate(pieces, axis=0))
        result = jnp.dot(
            back[...], jnp.concatenate(ups, axis=1), preferred_element_type=jnp.float32
        ).astype(jnp.bfloat16)
        for s in range(width):
            out[base + s, c] = result[:, s * LANE : (s + 1) * LANE]

    @pl.loop(0, items)
    def _(i):
        @pl.when(i % n > 0)
        def _():
            exchange(i).wait_send()

        @pl.when(tm < n_tm - 1)
        def _():
            forward(i).wait_send()


def settle(chunks, src, out, out_sem):
    size = src.shape[0] // chunks
    copies = [
        pltpu.make_async_copy(src.at[pl.ds(j * size, size)], out.at[pl.ds(j * size, size)], out_sem.at[j])
        for j in range(chunks)
    ]
    for copy in copies:
        copy.start()
    for copy in copies:
        copy.wait()


def body(volts, scales, dm_rate):
    lanes, seg_len = volts.shape[1], volts.shape[3]
    count = scales.shape[2]
    n, n_tm = lax.axis_size("chan"), lax.axis_size("tm")
    own = lanes // n
    width = 2 if own % 2 == 0 else 1
    rows = seg_len // LANE * 2
    values = volts.reshape(lanes, 2, seg_len // LANE, LANE).transpose(0, 2, 1, 3).reshape(lanes, rows, LANE)
    left, right, unright, back, twist = tables()
    items = n * (own // width)
    vmem = pl.BlockSpec(memory_space=pltpu.VMEM)
    hbm = pl.BlockSpec(memory_space=pltpu.MemorySpace.HBM)
    dma = pltpu.SemaphoreType.DMA
    out = pl.pallas_call(
        functools.partial(kernel, n, n_tm, own, width),
        out_shape=pltpu.VMEM((own, n, rows, LANE), jnp.bfloat16),
        in_specs=[pl.BlockSpec(memory_space=pltpu.SMEM), vmem] + [hbm] * 6,
        out_specs=vmem,
        scratch_shapes=[
            pltpu.VMEM((lanes, rows, LANE), jnp.bfloat16),
            pltpu.VMEM((n, own, rows, LANE), jnp.bfloat16),
            pltpu.VMEM((n, own, PRIOR, LANE), jnp.bfloat16),
        ]
        + [pltpu.VMEM(x.shape, x.dtype) for x in (left, right, unright, back, twist)]
        + [
            pltpu.VMEM((LANE, LANE), jnp.float32),
            pltpu.VMEM((rows, LANE), jnp.float32),
            dma((items,)),
            dma((5,)),
            dma((items,)),
            dma((items,)),
            dma((items,)),
            dma((items,)),
        ],
        compiler_params=pltpu.CompilerParams(
            collective_id=0, has_side_effects=True, vmem_limit_bytes=52 * 2**20
        ),
        name="dedisperse",
    )(dm_rate.transpose(0, 2, 1), scales.reshape(lanes, count), values, left, right, unright, back, twist)
    out = pl.pallas_call(
        functools.partial(settle, own),
        out_shape=jax.ShapeDtypeStruct((own * n, rows, LANE), jnp.bfloat16),
        in_specs=[vmem],
        out_specs=hbm,
        scratch_shapes=[dma((own,))],
        compiler_params=pltpu.CompilerParams(vmem_limit_bytes=16 * 2**20),
        name="settle",
    )(out.reshape(own * n, rows, LANE))
    out = out.reshape(own, n, seg_len // LANE, 2, LANE).transpose(0, 1, 3, 2, 4)
    return out.reshape(own, n, 2, seg_len)


def solution(mesh):
    return jax.shard_map(
        body,
        mesh=mesh,
        in_specs=(P("chan", None, None, "tm"), P("chan", None, "tm"), P()),
        out_specs=P("chan", None, None, "tm"),
        check_vma=False,
    )
```

```python
import functools
import math

import jax
import jax.numpy as jnp
import ml_dtypes
import numpy as np
from jax import lax
from jax.experimental import pallas as pl
from jax.experimental.pallas import tpu as pltpu
from jax.sharding import PartitionSpec as P

RADIX_A = 128
RADIX_B = 256
NFFT = RADIX_A * RADIX_B
INTERSECTION = 8192
LANE = 128
HALVES = RADIX_B // LANE
PRIOR = INTERSECTION // LANE * 2
MESH = pl.DeviceIdType.MESH


def dft_parts(radix):
    index = np.arange(radix)
    angle = 2.0 * np.pi / radix * (np.outer(index, index) % radix)
    rounded = lambda x: x.astype(np.float32).astype(ml_dtypes.bfloat16).astype(np.float32)
    return rounded(np.cos(angle)), rounded(-np.sin(angle))


def tables():
    are, aim = dft_parts(RADIX_A)
    bre, bim = dft_parts(RADIX_B)
    eye = np.eye(HALVES, dtype=np.float32)
    left = np.array([[are, -aim], [aim, are]])
    left = np.einsum("dckn,hg->hdkngc", left, eye).reshape(HALVES * 2 * RADIX_A, -1)
    back = np.array([[are, aim], [-aim, are]]) / NFFT
    back = np.einsum("dcnk,hg->nhdgck", back, eye).reshape(-1, HALVES * 2 * RADIX_A)
    back = back[PRIOR:]
    right = np.array([[bre, bim], [-bim, bre]])
    right = right.transpose(0, 2, 1, 3).reshape(2 * RADIX_B, 2 * RADIX_B)
    unright = np.array([[bre, -bim], [bim, bre]])
    unright = unright.transpose(0, 2, 1, 3).reshape(2 * RADIX_B, 2 * RADIX_B)
    turn = np.outer(np.arange(RADIX_A), np.arange(RADIX_B)) % NFFT
    angle = 2.0 * np.pi / NFFT * turn
    twist = np.stack([np.cos(angle), -np.sin(angle)]).astype(np.float32)
    half = lambda x: x.astype(ml_dtypes.bfloat16)
    return half(left), half(right), half(unright), half(back), twist


def chirp(rate):
    shape = (RADIX_A, RADIX_B)
    k = lax.broadcasted_iota(jnp.int32, shape, 0) + RADIX_A * lax.broadcasted_iota(jnp.int32, shape, 1)
    g = jnp.minimum(k, NFFT - k)
    phase = rate * (g * g) - (k << 29)
    quarter = (phase + (1 << 29)) >> 30
    x = (phase - (quarter << 30)).astype(jnp.float32) * (2.0 * math.pi / 2.0**32)
    y = x * x
    s = x + x * y * (-1.6666654611e-1 + y * (8.3321608736e-3 + y * -1.9515295891e-4))
    c = 1.0 + y * (-0.5 + y * (4.166664568298827e-2 + y * (-1.388731625493765e-3 + y * 2.443315711809948e-5)))
    odd = (quarter & 1) == 1
    re = jnp.where(odd, s, c)
    im = jnp.where(odd, c, s)
    re = jnp.where(((quarter + 1) & 2) == 2, -re, re)
    im = jnp.where((quarter & 2) == 2, -im, im)
    return re, im


def bitwise_xor(a, b, bits):
    total = 0
    for i in range(bits):
        total = total + (a // 2**i + b // 2**i) % 2 * 2**i
    return total


def kernel(n, n_tm, own, width, rates, scales, volts, left_in, right_in, unright_in, back_in, twist_in,
           out, values, got, tail, left, right, unright, back, twist, square, spread,
           load_sem, table_sem, send_sem, recv_sem, tail_send, tail_recv):
    me = lax.axis_index("chan")
    tm = lax.axis_index("tm")
    groups = own // width
    items = n * groups
    rows = values.shape[1]
    bits = (n - 1).bit_length()

    def place(i):
        return i // n, bitwise_xor(me, i % n, bits)

    def ahead(j):
        first = 1 - (j + items - n) // items
        return j + first * (n - 1 - 2 * j)

    def load(i):
        g, peer = place(i)
        at = pl.ds(peer * own + g * width, width)
        return pltpu.make_async_copy(volts.at[at], values.at[at], load_sem.at[i])

    fills = [
        pltpu.make_async_copy(src, dst, table_sem.at[j])
        for j, (src, dst) in enumerate(
            [(left_in, left), (twist_in, twist), (right_in, right), (unright_in, unright), (back_in, back)]
        )
    ]

    barrier = pltpu.get_barrier_semaphore()

    @pl.loop(1, n)
    def _(r):
        pl.semaphore_signal(barrier, inc=1, device_id={"chan": bitwise_xor(me, r, bits)}, device_id_type=MESH)

    pl.semaphore_signal(barrier, inc=1, device_id={"tm": (tm + n_tm - 1) % n_tm}, device_id_type=MESH)
    pl.semaphore_signal(barrier, inc=1, device_id={"tm": (tm + 1) % n_tm}, device_id_type=MESH)

    @pl.loop(0, items)
    def _(j):
        load(ahead(j)).start()

    for fill in fills:
        fill.start()

    lanes, count = scales.shape
    square[...] = jnp.zeros_like(square)
    square[0:lanes, 0:count] = scales[...]
    flipped = square[...].T[0:count]
    for j in range(rows // count):
        spread[pl.ds(j, count, stride=rows // count), :] = flipped

    pl.semaphore_wait(barrier, n + 1)

    def exchange(i):
        g, peer = place(i)
        return pltpu.make_async_remote_copy(
            src_ref=values.at[pl.ds(peer * own + g * width, width)],
            dst_ref=got.at[me, pl.ds(g * width, width)],
            send_sem=send_sem.at[i],
            recv_sem=recv_sem.at[i],
            device_id={"chan": peer},
            device_id_type=MESH,
        )

    def forward(i):
        g, peer = place(i)
        return pltpu.make_async_remote_copy(
            src_ref=got.at[peer, pl.ds(g * width, width), pl.ds(rows - PRIOR, PRIOR)],
            dst_ref=tail.at[peer, pl.ds(g * width, width)],
            send_sem=tail_send.at[i],
            recv_sem=tail_recv.at[i],
            device_id={"tm": tm + 1},
            device_id_type=MESH,
        )

    @pl.loop(0, items)
    def _(j):
        i = ahead(j)
        g, peer = place(i)
        load(i).wait()
        first = peer * own + g * width
        turned = pltpu.roll(spread[...], (LANE - first) % LANE, 1)
        for s in range(width):
            scale = jnp.broadcast_to(turned[:, s : s + 1], (rows, LANE))
            scaled = (values[first + s].astype(jnp.float32) * scale).astype(jnp.bfloat16)

            @pl.when(i % n > 0)
            def _():
                values[first + s] = scaled

            @pl.when(i % n == 0)
            def _():
                got[me, g * width + s] = scaled

        @pl.when(i % n > 0)
        def _():
            exchange(i).start()

    @pl.when(tm == 0)
    def _():
        @pl.loop(0, n)
        def _(c):
            tail[c] = jnp.zeros(tail.shape[1:], tail.dtype)

    for fill in fills:
        fill.wait()

    def advance(i):
        @pl.when(i % n > 0)
        def _():
            exchange(i).wait_recv()

        @pl.when(tm < n_tm - 1)
        def _():
            forward(i).start()

    advance(0)

    @pl.loop(0, items)
    def _(i):
        g, c = place(i)
        base = g * width
        lane = me * own + base
        cre, cim = chirp(rates[c, lane // 2 % 2, lane // 4])

        @pl.when(i + 1 < items)
        def _():
            advance(i + 1)

        @pl.when(tm > 0)
        def _():
            forward(i).wait_recv()

        wre, wim = twist[0], twist[1]
        streams = [
            jnp.concatenate([tail[c, base + s], got[c, base + s]], axis=0) for s in range(width)
        ]
        section = jnp.dot(
            left[...], jnp.concatenate(streams, axis=1), preferred_element_type=jnp.float32
        )
        ups = []
        for s in range(width):
            cols = slice(s * LANE, (s + 1) * LANE)
            part = lambda d: jnp.concatenate(
                [section[(h * 2 + d) * RADIX_A : (h * 2 + d + 1) * RADIX_A, cols] for h in range(HALVES)], axis=1
            )
            sre, sim = part(0), part(1)
            turned = jnp.concatenate(
                [(sre * wre - sim * wim).astype(jnp.bfloat16), (sre * wim + sim * wre).astype(jnp.bfloat16)], axis=1
            )
            spec = jnp.dot(turned, right[...], preferred_element_type=jnp.float32)
            sre, sim = spec[:, :RADIX_B], spec[:, RADIX_B:]
            shaped = jnp.concatenate(
                [(sre * cre - sim * cim).astype(jnp.bfloat16), (sre * cim + sim * cre).astype(jnp.bfloat16)], axis=1
            )
            spun = jnp.dot(shaped, unright[...], preferred_element_type=jnp.float32)
            sre, sim = spun[:, :RADIX_B], spun[:, RADIX_B:]
            ure = (sre * wre + sim * wim).astype(jnp.bfloat16)
            uim = (sim * wre - sre * wim).astype(jnp.bfloat16)
            pieces = []
            for h in range(HALVES):
                pieces += [ure[:, h * LANE : (h + 1) * LANE], uim[:, h * LANE : (h + 1) * LANE]]
            ups.append(jnp.concatenate(pieces, axis=0))
        result = jnp.dot(
            back[...], jnp.concatenate(ups, axis=1), preferred_element_type=jnp.float32
        ).astype(jnp.bfloat16)
        for s in range(width):
            out[base + s, c] = result[:, s * LANE : (s + 1) * LANE]

    @pl.loop(0, items)
    def _(i):
        @pl.when(i % n > 0)
        def _():
            exchange(i).wait_send()

        @pl.when(tm < n_tm - 1)
        def _():
            forward(i).wait_send()


def settle(chunks, src, out, out_sem):
    size = src.shape[0] // chunks
    copies = [
        pltpu.make_async_copy(src.at[pl.ds(j * size, size)], out.at[pl.ds(j * size, size)], out_sem.at[j])
        for j in range(chunks)
    ]
    for copy in copies:
        copy.start()
    for copy in copies:
        copy.wait()


def body(volts, scales, dm_rate):
    lanes, seg_len = volts.shape[1], volts.shape[3]
    count = scales.shape[2]
    n, n_tm = lax.axis_size("chan"), lax.axis_size("tm")
    own = lanes // n
    width = 2 if own % 2 == 0 else 1
    rows = seg_len // LANE * 2
    values = volts.reshape(lanes, 2, seg_len // LANE, LANE).transpose(0, 2, 1, 3).reshape(lanes, rows, LANE)
    left, right, unright, back, twist = tables()
    items = n * (own // width)
    vmem = pl.BlockSpec(memory_space=pltpu.VMEM)
    hbm = pl.BlockSpec(memory_space=pltpu.MemorySpace.HBM)
    dma = pltpu.SemaphoreType.DMA
    out = pl.pallas_call(
        functools.partial(kernel, n, n_tm, own, width),
        out_shape=pltpu.VMEM((own, n, rows, LANE), jnp.bfloat16),
        in_specs=[pl.BlockSpec(memory_space=pltpu.SMEM), vmem] + [hbm] * 6,
        out_specs=vmem,
        scratch_shapes=[
            pltpu.VMEM((lanes, rows, LANE), jnp.bfloat16),
            pltpu.VMEM((n, own, rows, LANE), jnp.bfloat16),
            pltpu.VMEM((n, own, PRIOR, LANE), jnp.bfloat16),
        ]
        + [pltpu.VMEM(x.shape, x.dtype) for x in (left, right, unright, back, twist)]
        + [
            pltpu.VMEM((LANE, LANE), jnp.float32),
            pltpu.VMEM((rows, LANE), jnp.float32),
            dma((items,)),
            dma((5,)),
            dma((items,)),
            dma((items,)),
            dma((items,)),
            dma((items,)),
        ],
        compiler_params=pltpu.CompilerParams(
            collective_id=0, has_side_effects=True, vmem_limit_bytes=52 * 2**20
        ),
        name="dedisperse",
    )(dm_rate.transpose(0, 2, 1), scales.reshape(lanes, count), values, left, right, unright, back, twist)
    out = pl.pallas_call(
        functools.partial(settle, own),
        out_shape=jax.ShapeDtypeStruct((own * n, rows, LANE), jnp.bfloat16),
        in_specs=[vmem],
        out_specs=hbm,
        scratch_shapes=[dma((own,))],
        compiler_params=pltpu.CompilerParams(vmem_limit_bytes=16 * 2**20),
        name="settle",
    )(out.reshape(own * n, rows, LANE))
    out = out.reshape(own, n, seg_len // LANE, 2, LANE).transpose(0, 1, 3, 2, 4)
    return out.reshape(own, n, 2, seg_len)


def solution(mesh):
    return jax.shard_map(
        body,
        mesh=mesh,
        in_specs=(P("chan", None, None, "tm"), P("chan", None, "tm"), P()),
        out_specs=P("chan", None, None, "tm"),
        check_vma=False,
    )
```
